256 devices in a mesh: section: 16 (over x_lo, y, core), dp: 16 (over x_hi, z).
Axes of the slice: x: 4 (x_hi: 2, x_lo: 2; x = x_hi * 2 + x_lo), y: 4, z: 8, core: 2. Of those that a mesh axis runs over, the one named last changes fastest.
Arguments:
- inputs: bfloat16 [32768, 8192], P(('section', 'dp')), may hold values from -6 to 6
- hidden_grad: bfloat16 [32768, 1024], P(('section', 'dp')), may hold values from -12 to 12
- gate_pre: bfloat16 [32768, 1024], P(('section', 'dp')), may hold values from -8 to 8
- up_weight: bfloat16 [131072, 1024], P(('section', 'dp')), may hold values from -0.1875 to 0.1875
- row_state: float32 [131072], P(('section', 'dp')), may hold values from 100 to 3000
- col_state: float32 [16384], P('section'), may hold values from 100 to 3000
Outputs:
- upstream: bfloat16 [32768, 8192], P(('section', 'dp'))
- param_step: bfloat16 [131072, 1024], P(('section', 'dp'))
- row_out: float32 [131072], P(('section', 'dp'))
- col_out: float32 [16384], P('section')
The draws below stay inside these ranges and needn't reach their ends.
All inputs are finite; a program needn't handle non-finite values.
Results may differ from the reference program's by a relative error of at most 0.0049.
Values may be sent and summed in bfloat16 or wider, within the bound.
A program may use at most 128 MiB of HBM per device.

```python
import math
import jax
import jax.numpy as jnp
from jax import lax

D = 8192
FF = 1024
TOKENS = 2048
N_SECTION = 16


def block_scale(rng, extent, cuts, smallest, high):
    level = 1.0
    for axis_at, shards_of in cuts:
        steps = jax.random.uniform(jax.random.fold_in(jax.random.fold_in(rng, 6), axis_at), (shards_of,), jnp.float32, smallest / len(cuts), high / len(cuts))
        level = level * jnp.repeat(jnp.exp(steps), extent[axis_at] // shards_of).reshape((-1,) + (1,) * (len(extent) - 1 - axis_at))
    return level


def scatter_about(own_key, extent, deviation, most, pieces=(), kind=jnp.bfloat16):
    values = jax.random.normal(own_key, extent, jnp.float32) * deviation
    if len(pieces) > 0:
        values = block_scale(own_key, extent, pieces, -0.22, 0.18) * values
    return jnp.clip(values, min=-most, max=most).astype(kind)


def setup_inputs(seed: int = 0) -> dict:
    key_of = jax.random.split(jax.random.key(seed), 7)
    inputs = scatter_about(key_of[0], (N_SECTION * TOKENS, D), 1.0, 6.0, ((0, 256),))
    hidden_grad = scatter_about(key_of[1], (N_SECTION * TOKENS, FF), 2.0, 12.0, ((0, 256),))
    gate_pre = scatter_about(key_of[2], (N_SECTION * TOKENS, FF), 1.5, 8.0, ((0, 256),))
    up_weight = scatter_about(key_of[3], (N_SECTION * D, FF), FF ** -0.5, 0.1875, ((0, 256),))
    row_state = jnp.clip(jnp.exp(math.log(3000.0) - 3.4011974 * jax.random.uniform(key_of[4], (N_SECTION * D,), jnp.float32) ** block_scale(key_of[4], (N_SECTION * D,), ((0, 256),), -0.2, 0.2)), 100.0, 3000.0)
    col_state = jnp.clip(jnp.exp(math.log(3000.0) - 3.4011974 * jax.random.uniform(key_of[5], (N_SECTION * FF,), jnp.float32) ** block_scale(key_of[5], (N_SECTION * FF,), ((0, 16),), -0.2, 0.2)), 100.0, 3000.0)
    return dict(inputs=inputs, hidden_grad=hidden_grad, gate_pre=gate_pre, up_weight=up_weight, row_state=row_state, col_state=col_state)


BETA_TWO = 0.75
TINY_ADD = 1e-30

def adafactor(gradient, row_state, col_state):
    squares = gradient * gradient + TINY_ADD
    row_new = BETA_TWO * row_state + (1.0 - BETA_TWO) * lax.optimization_barrier(jnp.mean(squares, axis=1))
    col_new = BETA_TWO * col_state + (1.0 - BETA_TWO) * lax.optimization_barrier(jnp.mean(squares, axis=0))
    second = row_new[:, None] * col_new[None, :] / jnp.mean(row_new)
    update = gradient / jnp.sqrt(second)
    root_mean = jnp.sqrt(jnp.mean(update * update))
    step_out = (update / jnp.maximum(1.0, root_mean)).astype(jnp.bfloat16)
    return (step_out, row_new, col_new)

def one_section(operands):
    inputs, hidden_grad, gate_pre, weight, row_state, col_state = operands
    cotangent = (hidden_grad.astype(jnp.float32) * jax.nn.silu(gate_pre.astype(jnp.float32))).astype(jnp.bfloat16)
    lowered = jnp.dot(cotangent, weight.T, preferred_element_type=jnp.float32).astype(jnp.bfloat16)
    gradient = jnp.dot(inputs.T, cotangent, preferred_element_type=jnp.float32)
    step_out, row_new, col_new = adafactor(gradient, row_state, col_state)
    return (lowered, step_out, row_new, col_new)

def reference(inputs, hidden_grad, gate_pre, up_weight, row_state, col_state):
    stacked = (inputs.reshape(N_SECTION, TOKENS, D), hidden_grad.reshape(N_SECTION, TOKENS, FF), gate_pre.reshape(N_SECTION, TOKENS, FF), up_weight.reshape(N_SECTION, D, FF), row_state.reshape(N_SECTION, D), col_state.reshape(N_SECTION, FF))
    lowered, step_out, row_new, col_new = lax.map(one_section, stacked)
    upstream = jnp.concatenate([lowered[1:], jnp.zeros((1, TOKENS, D), jnp.bfloat16)], axis=0)
    return (upstream.reshape(N_SECTION * TOKENS, D), step_out.reshape(N_SECTION * D, FF), row_new.reshape(N_SECTION * D), col_new.reshape(N_SECTION * FF))
```

```python
import functools

import jax
import jax.numpy as jnp
from jax import lax
from jax.experimental import pallas as pl
from jax.experimental.pallas import tpu as pltpu
from jax.sharding import PartitionSpec as P

D = 8192
FF = 1024
TOK = 128
ROWS = 512
NZ = 8
BETA_TWO = 0.75
TINY_ADD = 1e-30
LAST = 15

MESH = pl.DeviceIdType.MESH
BF = jnp.bfloat16
F32 = jnp.float32

NEAR_FIRST = (1, 7, 2, 6, 3, 5, 4)
FAR_FIRST = (4, 3, 5, 2, 6, 1, 7)


def body(
    x_hbm, hg_hbm, gp_hbm, w_hbm, rstate_hbm, cstate_hbm,
    up_out, step_out, row_out, col_out,
    hg, gp, ctg, w2, xr, lo, grad, gsend, grecv, stepb, rcol, rvec, cvec, smine, spair, sall, zbuf,
    lsem, ag_s, ag_r, w_s, w_r, x_s, x_r, l_s, l_r, g_s, g_r, p_s, p_r, s_s, s_r, o_s, z_s,
):
    s = lax.axis_index("section")
    dp = lax.axis_index("dp")
    xh, z = dp // NZ, dp % NZ

    def ring(k):
        return (z + k) % NZ

    def device(section, half, zz):
        return {"section": section, "dp": half * NZ + zz}

    def remote(src, dst, send, recv, target):
        return pltpu.make_async_remote_copy(
            src_ref=src, dst_ref=dst, send_sem=send, recv_sem=recv, device_id=target, device_id_type=MESH
        )

    barrier = pltpu.get_barrier_semaphore()
    for k in range(1, NZ):
        pl.semaphore_signal(barrier, inc=1, device_id=device(s, xh, ring(k)), device_id_type=MESH)
    pl.semaphore_signal(barrier, inc=1, device_id=device(s, 1 - xh, z), device_id_type=MESH)

    @pl.when(s < LAST)
    def _():
        for k in range(NZ):
            pl.semaphore_signal(barrier, inc=1, device_id=device(s + 1, xh, ring(k)), device_id_type=MESH)

    def columns(half, zz):
        return pl.ds(pl.multiple_of((half * NZ + zz) * ROWS, ROWS), ROWS)

    loads = [
        pltpu.make_async_copy(hg_hbm, hg, lsem.at[0]),
        pltpu.make_async_copy(gp_hbm, gp, lsem.at[1]),
        pltpu.make_async_copy(w_hbm, w2.at[0], lsem.at[2]),
        pltpu.make_async_copy(x_hbm.at[:, columns(1 - xh, z)], xr.at[0, z], lsem.at[3]),
        pltpu.make_async_copy(x_hbm.at[:, columns(xh, z)], xr.at[1, z], lsem.at[4]),
        pltpu.make_async_copy(rstate_hbm, rvec, lsem.at[5]),
        pltpu.make_async_copy(cstate_hbm, cvec, lsem.at[6]),
    ]
    for load in loads:
        load.start()
    loads[0].wait()
    loads[1].wait()

    @pl.loop(0, 4)
    def _(i):
        rows = pl.ds(pl.multiple_of(i * 32, 32), 32)
        v = gp[rows, :].astype(F32)
        ctg[z, rows, :] = (hg[rows, :].astype(F32) * (v / (1.0 + jnp.exp(-v)))).astype(BF)

    pl.semaphore_wait(barrier, NZ + NZ * (s > 0).astype(jnp.int32))

    def gather_step(step):
        copies = []
        for way, d in ((0, 1), (1, -1)):
            block = (z + NZ - d * step) % NZ
            if step < 3:
                ref = ctg.at[block]
            else:
                ref = ctg.at[block, pl.ds(way * (TOK // 2), TOK // 2)]
            copies.append(remote(ref, ref, ag_s.at[way, step], ag_r.at[way, step], device(s, xh, (z + NZ + d) % NZ)))
        return copies

    gathers = [gather_step(step) for step in range(4)]
    weights = remote(w_hbm, w2.at[1], w_s, w_r, device(s, 1 - xh, z))

    def inputs_copy(slot, k):
        half = 1 - xh if slot == 0 else xh
        return remote(
            x_hbm.at[:, columns(half, ring(k))], xr.at[slot, z], x_s.at[slot, k], x_r.at[slot, k], device(s, xh, ring(k))
        )

    inputs_copies = [[inputs_copy(slot, k) for k in FAR_FIRST] for slot in range(2)]

    def lowered_copy(slot, k):
        half = xh if slot == 0 else 1 - xh
        return remote(lo.at[slot, k], up_out.at[:, columns(half, z)], l_s.at[slot, k], l_r.at[slot, k], device(s - 1, xh, ring(k)))

    def lowered(slot, k):
        lo[slot, k] = lax.dot_general(
            ctg[ring(k)], w2[slot], (((1,), (1,)), ((), ())), preferred_element_type=F32
        ).astype(BF)

        @pl.when(s > 0)
        def _():
            lowered_copy(slot, k).start()

    for copy in gathers[0]:
        copy.start()
    weights.start()
    for copy in inputs_copies[0]:
        copy.start()

    zbuf[...] = jnp.zeros_like(zbuf)

    @pl.when(s == LAST)
    def _():
        for i in range(NZ):
            pltpu.make_async_copy(zbuf, up_out.at[:, pl.ds(i * 2 * ROWS, 2 * ROWS)], z_s.at[i]).start()

    loads[2].wait()
    lowered(0, 0)
    for step in range(4):
        for copy in gathers[step]:
            copy.wait_recv()
        if step < 3:
            for copy in gathers[step + 1]:
                copy.start()
        if step == 1:
            for copy in inputs_copies[1]:
                copy.start()
        for k in ((step + 1, NZ - 1 - step) if step < 3 else (4,)):
            lowered(0, k)

    weights.wait_recv()
    for k in (0,) + NEAR_FIRST:
        lowered(1, k)

    def gradient(slot, store):
        for part in range(2):
            cols = pl.ds(part * 256, 256)
            xs = xr[slot, :, :, cols].reshape(NZ * TOK, 256)
            ct = ctg[...].reshape(NZ * TOK, FF)
            store(cols, lax.dot_general(xs, ct, (((0,), (0,)), ((), ())), preferred_element_type=F32))

    for copy in inputs_copies[0]:
        copy.wait_recv()
    loads[3].wait()

    def store_send(rows, value):
        gsend[rows, :] = value.astype(BF)

    gradient(0, store_send)
    partial = remote(gsend, grecv, g_s, g_r, device(s, 1 - xh, z))
    partial.start()

    loads[5].wait()
    loads[6].wait()
    for q in range(4):
        rcol[pl.ds(q * 128, 128), :] = jnp.transpose(jnp.broadcast_to(rvec[pl.ds(q, 1), :], (128, 128)))

    for copy in inputs_copies[1]:
        copy.wait_recv()
    loads[4].wait()

    def store_own(rows, value):
        grad[rows, :] = value

    gradient(1, store_own)
    partial.wait_recv()

    def tile(q):
        return pl.ds(pl.multiple_of(q * 128, 128), 128)

    def squares_step(q, rowsum):
        g = grad[:, tile(q)] + grecv[:, tile(q)].astype(F32)
        grad[:, tile(q)] = g
        sq = g * g + TINY_ADD
        smine[pl.ds(q, 1), :] = jnp.sum(sq, axis=0, keepdims=True)
        return rowsum + sq

    rowsum = lax.fori_loop(0, 8, squares_step, jnp.zeros((ROWS, 128), F32))
    rowmean = jnp.sum(rowsum, axis=1, keepdims=True) * (1.0 / FF)
    rnew = BETA_TWO * rcol[...] + (1.0 - BETA_TWO) * jnp.broadcast_to(rowmean, (ROWS, 128))
    rcol[...] = rnew
    rinv = 1.0 / rnew

    def weighted_step(q, carry):
        g = grad[:, tile(q)]
        smine[pl.ds(8 + q, 1), :] = jnp.sum(g * g * rinv, axis=0, keepdims=True)
        return carry

    lax.fori_loop(0, 8, weighted_step, 0)
    smine[pl.ds(16, 8), :] = jnp.broadcast_to(jnp.sum(rnew, axis=0, keepdims=True), (8, 128))

    pair = remote(smine, spair, p_s, p_r, device(s, 1 - xh, z))
    pair.start()
    for q in range(4):
        rvec[pl.ds(q, 1), :] = jnp.transpose(rcol[pl.ds(q * 128, 128), :])[0:1, :]
    row_copy = pltpu.make_async_copy(rvec, row_out, o_s.at[0])
    row_copy.start()
    pair.wait_recv()
    sall[0] = smine[...] + spair[...]
    sums = [remote(sall.at[0], sall.at[k], s_s.at[k], s_r.at[k], device(s, xh, ring(k))) for k in FAR_FIRST]
    for copy in sums:
        copy.start()
    for copy in sums:
        copy.wait_recv()
    total = sall[(NZ - 0 + z) % NZ]
    for i in range(1, NZ):
        total = total + sall[(NZ - i + z) % NZ]
    cnew = BETA_TWO * cvec[...] + (1.0 - BETA_TWO) * (total[0:8] * (1.0 / D))
    cvec[...] = cnew
    col_copy = pltpu.make_async_copy(cvec, col_out, o_s.at[1])
    col_copy.start()
    average = total[16:17, :] * (1.0 / D)
    ratio = jnp.sum(jnp.sum(total[8:16] / cnew, axis=0, keepdims=True), axis=1, keepdims=True)
    root = jnp.sqrt(jnp.broadcast_to(ratio, (1, 128)) * average * (1.0 / (float(D) * float(FF))))
    scale = jnp.sqrt(average) / jnp.maximum(1.0, root)
    rowfac = lax.rsqrt(rcol[...]) * scale
    smine_free = lax.rsqrt(cnew)
    spair[pl.ds(0, 8), :] = smine_free

    def update_step(q, carry):
        stepb[:, tile(q)] = (grad[:, tile(q)] * rowfac * spair[pl.ds(q, 1), :]).astype(BF)
        return carry

    lax.fori_loop(0, 8, update_step, 0)
    step_copy = pltpu.make_async_copy(stepb, step_out, o_s.at[2])
    step_copy.start()

    for copies in gathers:
        for copy in copies:
            copy.wait_send()
    weights.wait_send()
    for copies in inputs_copies:
        for copy in copies:
            copy.wait_send()
    partial.wait_send()
    pair.wait_send()
    for copy in sums:
        copy.wait_send()

    @pl.when(s > 0)
    def _():
        for slot in range(2):
            for k in range(NZ):
                lowered_copy(slot, k).wait_send()

    @pl.when(s < LAST)
    def _():
        for slot in range(2):
            for k in range(NZ):
                lowered_copy(slot, k).wait_recv()

    @pl.when(s == LAST)
    def _():
        for i in range(NZ):
            pltpu.make_async_copy(zbuf, up_out.at[:, pl.ds(i * 2 * ROWS, 2 * ROWS)], z_s.at[i]).wait()

    row_copy.wait()
    col_copy.wait()
    step_copy.wait()


def local(inputs, hidden_grad, gate_pre, up_weight, row_state, col_state):
    hbm = pl.BlockSpec(memory_space=pl.ANY)
    dma = pltpu.SemaphoreType.DMA
    upstream, step_out, row_new, col_new = pl.pallas_call(
        body,
        name="relay_step",
        out_shape=(
            jax.ShapeDtypeStruct((TOK, D), BF),
            jax.ShapeDtypeStruct((ROWS, FF), BF),
            jax.ShapeDtypeStruct((ROWS // 128, 128), F32),
            jax.ShapeDtypeStruct((FF // 128, 128), F32),
        ),
        in_specs=[hbm] * 6,
        out_specs=(hbm,) * 4,
        scratch_shapes=[
            pltpu.VMEM((TOK, FF), BF),
            pltpu.VMEM((TOK, FF), BF),
            pltpu.VMEM((NZ, TOK, FF), BF),
            pltpu.VMEM((2, ROWS, FF), BF),
            pltpu.VMEM((2, NZ, TOK, ROWS), BF),
            pltpu.VMEM((2, NZ, TOK, ROWS), BF),
            pltpu.VMEM((ROWS, FF), F32),
            pltpu.VMEM((ROWS, FF), BF),
            pltpu.VMEM((ROWS, FF), BF),
            pltpu.VMEM((ROWS, FF), BF),
            pltpu.VMEM((ROWS, 128), F32),
            pltpu.VMEM((ROWS // 128, 128), F32),
            pltpu.VMEM((FF // 128, 128), F32),
            pltpu.VMEM((24, 128), F32),
            pltpu.VMEM((24, 128), F32),
            pltpu.VMEM((NZ, 24, 128), F32),
            pltpu.VMEM((TOK, 2 * ROWS), BF),
            dma((7,)),
            dma((2, 4)), dma((2, 4)),
            dma(()), dma(()),
            dma((2, NZ)), dma((2, NZ)),
            dma((2, NZ)), dma((2, NZ)),
            dma(()), dma(()),
            dma(()), dma(()),
            dma((NZ,)), dma((NZ,)),
            dma((3,)),
            dma((NZ,)),
        ],
        compiler_params=pltpu.CompilerParams(collective_id=0, has_side_effects=True, vmem_limit_bytes=32 << 20),
        cost_estimate=pl.CostEstimate(flops=4 * 1024 * 1024 * 1024, transcendentals=TOK * FF, bytes_accessed=8 << 20),
    )(
        inputs, hidden_grad, gate_pre, up_weight,
        row_state.reshape(ROWS // 128, 128), col_state.reshape(FF // 128, 128),
    )
    return upstream, step_out, row_new.reshape(ROWS), col_new.reshape(FF)


def solution(mesh):
    rows = P(("section", "dp"), None)
    placed = (rows, rows, rows, rows, P(("section", "dp")), P("section"))
    return jax.shard_map(
        local,
        mesh=mesh,
        in_specs=placed,
        out_specs=(rows, rows, P(("section", "dp")), P("section")),
        check_vma=False,
    )
```

```python
import functools

import jax
import jax.numpy as jnp
from jax import lax
from jax.experimental import pallas as pl
from jax.experimental.pallas import tpu as pltpu
from jax.sharding import PartitionSpec as P

D = 8192
FF = 1024
TOK = 128
ROWS = 512
NZ = 8
BETA_TWO = 0.75
TINY_ADD = 1e-30
LAST = 15

MESH = pl.DeviceIdType.MESH
BF = jnp.bfloat16
F32 = jnp.float32

NEAR_FIRST = (1, 7, 2, 6, 3, 5, 4)
FAR_FIRST = (4, 3, 5, 2, 6, 1, 7)


def body(
    x_hbm, hg_hbm, gp_hbm, w_hbm, rstate_hbm, cstate_hbm,
    up_out, step_out, row_out, col_out,
    hg, gp, ctg, w2, xr, lo, grad, gsend, grecv, stepb, rcol, rvec, cvec, smine, spair, sall, zbuf,
    lsem, ag_s, ag_r, w_s, w_r, x_s, x_r, l_s, l_r, g_s, g_r, p_s, p_r, s_s, s_r, o_s, z_s,
):
    s = lax.axis_index("section")
    dp = lax.axis_index("dp")
    xh, z = dp // NZ, dp % NZ

    def ring(k):
        return (z + k) % NZ

    def device(section, half, zz):
        return {"section": section, "dp": half * NZ + zz}

    def remote(src, dst, send, recv, target):
        return pltpu.make_async_remote_copy(
            src_ref=src, dst_ref=dst, send_sem=send, recv_sem=recv, device_id=target, device_id_type=MESH
        )

    barrier = pltpu.get_barrier_semaphore()
    for k in range(1, NZ):
        pl.semaphore_signal(barrier, inc=1, device_id=device(s, xh, ring(k)), device_id_type=MESH)
    pl.semaphore_signal(barrier, inc=1, device_id=device(s, 1 - xh, z), device_id_type=MESH)

    @pl.when(s < LAST)
    def _():
        for k in range(NZ):
            pl.semaphore_signal(barrier, inc=1, device_id=device(s + 1, xh, ring(k)), device_id_type=MESH)

    def columns(half, zz):
        return pl.ds(pl.multiple_of((half * NZ + zz) * ROWS, ROWS), ROWS)

    loads = [
        pltpu.make_async_copy(hg_hbm, hg, lsem.at[0]),
        pltpu.make_async_copy(gp_hbm, gp, lsem.at[1]),
        pltpu.make_async_copy(w_hbm, w2.at[0], lsem.at[2]),
        pltpu.make_async_copy(x_hbm.at[:, columns(1 - xh, z)], xr.at[0, z], lsem.at[3]),
        pltpu.make_async_copy(x_hbm.at[:, columns(xh, z)], xr.at[1, z], lsem.at[4]),
        pltpu.make_async_copy(rstate_hbm, rvec, lsem.at[5]),
        pltpu.make_async_copy(cstate_hbm, cvec, lsem.at[6]),
    ]
    for load in loads:
        load.start()
    loads[0].wait()
    loads[1].wait()

    @pl.loop(0, 4)
    def _(i):
        rows = pl.ds(pl.multiple_of(i * 32, 32), 32)
        v = gp[rows, :].astype(F32)
        ctg[z, rows, :] = (hg[rows, :].astype(F32) * (v / (1.0 + jnp.exp(-v)))).astype(BF)

    pl.semaphore_wait(barrier, NZ + NZ * (s > 0).astype(jnp.int32))

    def gather_step(step):
        copies = []
        for way, d in ((0, 1), (1, -1)):
            block = (z + NZ - d * step) % NZ
            if step < 3:
                ref = ctg.at[block]
            else:
                ref = ctg.at[block, pl.ds(way * (TOK // 2), TOK // 2)]
            copies.append(remote(ref, ref, ag_s.at[way, step], ag_r.at[way, step], device(s, xh, (z + NZ + d) % NZ)))
        return copies

    gathers = [gather_step(step) for step in range(4)]
    weights = remote(w_hbm, w2.at[1], w_s, w_r, device(s, 1 - xh, z))

    def inputs_copy(slot, k):
        half = 1 - xh if slot == 0 else xh
        return remote(
            x_hbm.at[:, columns(half, ring(k))], xr.at[slot, z], x_s.at[slot, k], x_r.at[slot, k], device(s, xh, ring(k))
        )

    inputs_copies = [[inputs_copy(slot, k) for k in FAR_FIRST] for slot in range(2)]

    def lowered_copy(slot, k):
        half = xh if slot == 0 else 1 - xh
        return remote(lo.at[slot, k], up_out.at[:, columns(half, z)], l_s.at[slot, k], l_r.at[slot, k], device(s - 1, xh, ring(k)))

    def lowered(slot, k):
        lo[slot, k] = lax.dot_general(
            ctg[ring(k)], w2[slot], (((1,), (1,)), ((), ())), preferred_element_type=F32
        ).astype(BF)

        @pl.when(s > 0)
        def _():
            lowered_copy(slot, k).start()

    for copy in gathers[0]:
        copy.start()
    weights.start()
    for copy in inputs_copies[0]:
        copy.start()

    zbuf[...] = jnp.zeros_like(zbuf)

    @pl.when(s == LAST)
    def _():
        for i in range(NZ):
            pltpu.make_async_copy(zbuf, up_out.at[:, pl.ds(i * 2 * ROWS, 2 * ROWS)], z_s.at[i]).start()

    loads[2].wait()
    lowered(0, 0)
    for step in range(4):
        for copy in gathers[step]:
            copy.wait_recv()
        if step < 3:
            for copy in gathers[step + 1]:
                copy.start()
        if step == 3:
            for copy in inputs_copies[1]:
                copy.start()
        for k in ((step + 1, NZ - 1 - step) if step < 3 else (4,)):
            lowered(0, k)

    def gradient(slot, store):
        for part in range(2):
            cols = pl.ds(part * 256, 256)
            xs = xr[slot, :, :, cols].reshape(NZ * TOK, 256)
            ct = ctg[...].reshape(NZ * TOK, FF)
            store(cols, lax.dot_general(xs, ct, (((0,), (0,)), ((), ())), preferred_element_type=F32))

    for copy in inputs_copies[0]:
        copy.wait_recv()
    loads[3].wait()

    def store_send(rows, value):
        gsend[rows, :] = value.astype(BF)

    gradient(0, store_send)
    partial = remote(gsend, grecv, g_s, g_r, device(s, 1 - xh, z))
    partial.start()

    weights.wait_recv()
    for k in (0,) + NEAR_FIRST:
        lowered(1, k)

    loads[5].wait()
    loads[6].wait()
    for q in range(4):
        rcol[pl.ds(q * 128, 128), :] = jnp.transpose(jnp.broadcast_to(rvec[pl.ds(q, 1), :], (128, 128)))

    for copy in inputs_copies[1]:
        copy.wait_recv()
    loads[4].wait()

    def store_own(rows, value):
        grad[rows, :] = value

    gradient(1, store_own)
    partial.wait_recv()

    def tile(q):
        return pl.ds(pl.multiple_of(q * 128, 128), 128)

    def squares_step(q, rowsum):
        g = grad[:, tile(q)] + grecv[:, tile(q)].astype(F32)
        grad[:, tile(q)] = g
        sq = g * g + TINY_ADD
        smine[pl.ds(q, 1), :] = jnp.sum(sq, axis=0, keepdims=True)
        return rowsum + sq

    rowsum = lax.fori_loop(0, 8, squares_step, jnp.zeros((ROWS, 128), F32))
    rowmean = jnp.sum(rowsum, axis=1, keepdims=True) * (1.0 / FF)
    rnew = BETA_TWO * rcol[...] + (1.0 - BETA_TWO) * jnp.broadcast_to(rowmean, (ROWS, 128))
    rcol[...] = rnew
    rinv = 1.0 / rnew

    def weighted_step(q, carry):
        g = grad[:, tile(q)]
        smine[pl.ds(8 + q, 1), :] = jnp.sum(g * g * rinv, axis=0, keepdims=True)
        return carry

    lax.fori_loop(0, 8, weighted_step, 0)
    smine[pl.ds(16, 8), :] = jnp.broadcast_to(jnp.sum(rnew, axis=0, keepdims=True), (8, 128))

    pair = remote(smine, spair, p_s, p_r, device(s, 1 - xh, z))
    pair.start()
    for q in range(4):
        rvec[pl.ds(q, 1), :] = jnp.transpose(rcol[pl.ds(q * 128, 128), :])[0:1, :]
    row_copy = pltpu.make_async_copy(rvec, row_out, o_s.at[0])
    row_copy.start()
    pair.wait_recv()
    sall[0] = smine[...] + spair[...]
    sums = [remote(sall.at[0], sall.at[k], s_s.at[k], s_r.at[k], device(s, xh, ring(k))) for k in FAR_FIRST]
    for copy in sums:
        copy.start()
    for copy in sums:
        copy.wait_recv()
    total = sall[(NZ - 0 + z) % NZ]
    for i in range(1, NZ):
        total = total + sall[(NZ - i + z) % NZ]
    cnew = BETA_TWO * cvec[...] + (1.0 - BETA_TWO) * (total[0:8] * (1.0 / D))
    cvec[...] = cnew
    col_copy = pltpu.make_async_copy(cvec, col_out, o_s.at[1])
    col_copy.start()
    average = total[16:17, :] * (1.0 / D)
    ratio = jnp.sum(jnp.sum(total[8:16] / cnew, axis=0, keepdims=True), axis=1, keepdims=True)
    root = jnp.sqrt(jnp.broadcast_to(ratio, (1, 128)) * average * (1.0 / (float(D) * float(FF))))
    scale = jnp.sqrt(average) / jnp.maximum(1.0, root)
    rowfac = lax.rsqrt(rcol[...]) * scale
    smine_free = lax.rsqrt(cnew)
    spair[pl.ds(0, 8), :] = smine_free

    def update_step(q, carry):
        stepb[:, tile(q)] = (grad[:, tile(q)] * rowfac * spair[pl.ds(q, 1), :]).astype(BF)
        return carry

    lax.fori_loop(0, 8, update_step, 0)
    step_copy = pltpu.make_async_copy(stepb, step_out, o_s.at[2])
    step_copy.start()

    for copies in gathers:
        for copy in copies:
            copy.wait_send()
    weights.wait_send()
    for copies in inputs_copies:
        for copy in copies:
            copy.wait_send()
    partial.wait_send()
    pair.wait_send()
    for copy in sums:
        copy.wait_send()

    @pl.when(s > 0)
    def _():
        for slot in range(2):
            for k in range(NZ):
                lowered_copy(slot, k).wait_send()

    @pl.when(s < LAST)
    def _():
        for slot in range(2):
            for k in range(NZ):
                lowered_copy(slot, k).wait_recv()

    @pl.when(s == LAST)
    def _():
        for i in range(NZ):
            pltpu.make_async_copy(zbuf, up_out.at[:, pl.ds(i * 2 * ROWS, 2 * ROWS)], z_s.at[i]).wait()

    row_copy.wait()
    col_copy.wait()
    step_copy.wait()


def place(*refs):
    ins, outs, sem = refs[:4], refs[4:8], refs[8]
    copies = [pltpu.make_async_copy(a, b, sem.at[i]) for i, (a, b) in enumerate(zip(ins, outs))]
    for copy in copies:
        copy.start()
    for copy in copies:
        copy.wait()


def local(inputs, hidden_grad, gate_pre, up_weight, row_state, col_state):
    hbm = pl.BlockSpec(memory_space=pl.ANY)
    dma = pltpu.SemaphoreType.DMA
    upstream, step_out, row_new, col_new = pl.pallas_call(
        body,
        name="relay_step",
        out_shape=(
            jax.ShapeDtypeStruct((TOK, D), BF),
            jax.ShapeDtypeStruct((ROWS, FF), BF),
            jax.ShapeDtypeStruct((ROWS // 128, 128), F32),
            jax.ShapeDtypeStruct((FF // 128, 128), F32),
        ),
        in_specs=[hbm] * 6,
        out_specs=(hbm,) * 4,
        scratch_shapes=[
            pltpu.VMEM((TOK, FF), BF),
            pltpu.VMEM((TOK, FF), BF),
            pltpu.VMEM((NZ, TOK, FF), BF),
            pltpu.VMEM((2, ROWS, FF), BF),
            pltpu.VMEM((2, NZ, TOK, ROWS), BF),
            pltpu.VMEM((2, NZ, TOK, ROWS), BF),
            pltpu.VMEM((ROWS, FF), F32),
            pltpu.VMEM((ROWS, FF), BF),
            pltpu.VMEM((ROWS, FF), BF),
            pltpu.VMEM((ROWS, FF), BF),
            pltpu.VMEM((ROWS, 128), F32),
            pltpu.VMEM((ROWS // 128, 128), F32),
            pltpu.VMEM((FF // 128, 128), F32),
            pltpu.VMEM((24, 128), F32),
            pltpu.VMEM((24, 128), F32),
            pltpu.VMEM((NZ, 24, 128), F32),
            pltpu.VMEM((TOK, 2 * ROWS), BF),
            dma((7,)),
            dma((2, 4)), dma((2, 4)),
            dma(()), dma(()),
            dma((2, NZ)), dma((2, NZ)),
            dma((2, NZ)), dma((2, NZ)),
            dma(()), dma(()),
            dma(()), dma(()),
            dma((NZ,)), dma((NZ,)),
            dma((3,)),
            dma((NZ,)),
        ],
        compiler_params=pltpu.CompilerParams(collective_id=0, has_side_effects=True, vmem_limit_bytes=32 << 20),
        cost_estimate=pl.CostEstimate(flops=4 * 1024 * 1024 * 1024, transcendentals=TOK * FF, bytes_accessed=8 << 20),
    )(
        *(
            pltpu.with_memory_space_constraint(v, pltpu.HBM)
            for v in (inputs, hidden_grad, gate_pre, up_weight, row_state.reshape(ROWS // 128, 128), col_state.reshape(FF // 128, 128))
        )
    )
    results = (upstream, step_out, row_new, col_new)
    upstream, step_out, row_new, col_new = pl.pallas_call(
        place,
        name="place_outputs",
        out_shape=tuple(jax.ShapeDtypeStruct(v.shape, v.dtype) for v in results),
        in_specs=[hbm] * 4,
        out_specs=tuple([pl.BlockSpec(memory_space=pltpu.HBM)] * 4),
        scratch_shapes=[dma((4,))],
        compiler_params=pltpu.CompilerParams(vmem_limit_bytes=1 << 20),
    )(*results)
    return upstream, step_out, row_new.reshape(ROWS), col_new.reshape(FF)


def solution(mesh):
    rows = P(("section", "dp"), None)
    placed = (rows, rows, rows, rows, P(("section", "dp")), P("section"))
    return jax.shard_map(
        local,
        mesh=mesh,
        in_specs=placed,
        out_specs=(rows, rows, P(("section", "dp")), P("section")),
        check_vma=False,
    )
```

```python
import functools

import jax
import jax.numpy as jnp
from jax import lax
from jax.experimental import pallas as pl
from jax.experimental.pallas import tpu as pltpu
from jax.sharding import PartitionSpec as P

D = 8192
FF = 1024
TOK = 128
ROWS = 512
NZ = 8
BETA_TWO = 0.75
TINY_ADD = 1e-30
LAST = 15

GROUPS = (
    ((0, 4),), ((1, 4),), ((0, 3), (0, 1)), ((0, 5), (0, 7)), ((1, 3), (1, 1)), ((1, 5), (1, 7)), ((0, 2), (0, 6)), ((1, 2), (1, 6)),
)
GROUP_OF = {pair: i for i, group in enumerate(GROUPS) for pair in group}

MESH = pl.DeviceIdType.MESH
BF = jnp.bfloat16
F32 = jnp.float32

NEAR_FIRST = (1, 7, 2, 6, 3, 5, 4)
FAR_FIRST = (4, 3, 5, 2, 6, 1, 7)
INPUT_ORDER = (((0, 1), (0, 7), (1, 1), (1, 7)), ((0, 2), (0, 6)), ((0, 3), (0, 5)), ((0, 4), (1, 4), (1, 3), (1, 5), (1, 2), (1, 6)), ())
ORDER = tuple((slot, k) for slot in range(2) for k in FAR_FIRST)


def body(
    x_hbm, hg_hbm, gp_hbm, w_hbm, rstate_hbm, cstate_hbm,
    up_out, step_out, row_out, col_out,
    hg, gp, ctg, w2, xr, lo, grad, gsend, grecv, rcol, rvec, cvec, smine, sred, sgat, zbuf, passed,
    lsem, ag_s, ag_r, w_s, w_r, x_s, x_r, l_s, l_r, g_s, g_r, p_s, p_r, s_s, s_r, z_s, r_r, f_s, ready,
):
    s = lax.axis_index("section")
    dp = lax.axis_index("dp")
    xh, z = dp // NZ, dp % NZ

    def ring(k):
        return (z + k) % NZ

    def device(section, half, zz):
        return {"section": section, "dp": half * NZ + zz}

    def remote(src, dst, send, recv, target):
        return pltpu.make_async_remote_copy(
            src_ref=src, dst_ref=dst, send_sem=send, recv_sem=recv, device_id=target, device_id_type=MESH
        )

    barrier = pltpu.get_barrier_semaphore()
    def greet(sem, target):
        pl.semaphore_signal(sem, inc=1, device_id=target, device_id_type=MESH)

    for k in (1, NZ - 1):
        greet(barrier, device(s, xh, ring(k)))
    greet(barrier, device(s, 1 - xh, z))

    @pl.when(s < LAST)
    def _():
        greet(barrier, device(s + 1, xh, z))

    @pl.when(s > 0)
    def _():
        greet(barrier, device(s - 1, xh, z))

    def columns(half, zz):
        return pl.ds(pl.multiple_of((half * NZ + zz) * ROWS, ROWS), ROWS)

    loads = [
        pltpu.make_async_copy(hg_hbm, hg, lsem.at[0]),
        pltpu.make_async_copy(gp_hbm, gp, lsem.at[1]),
        pltpu.make_async_copy(w_hbm, w2.at[0], lsem.at[2]),
        pltpu.make_async_copy(x_hbm.at[:, columns(1 - xh, z)], xr.at[0, z], lsem.at[3]),
        pltpu.make_async_copy(x_hbm.at[:, columns(xh, z)], xr.at[1, z], lsem.at[4]),
        pltpu.make_async_copy(rstate_hbm, rvec, lsem.at[5]),
        pltpu.make_async_copy(cstate_hbm, cvec, lsem.at[6]),
    ]
    for load in loads:
        load.start()
    loads[0].wait()
    loads[1].wait()

    @pl.loop(0, 4)
    def _(i):
        rows = pl.ds(pl.multiple_of(i * 32, 32), 32)
        v = gp[rows, :].astype(F32)
        ctg[z, rows, :] = (hg[rows, :].astype(F32) * (v / (1.0 + jnp.exp(-v)))).astype(BF)

    pl.semaphore_wait(barrier, 3 + (s > 0).astype(jnp.int32) + (s < LAST).astype(jnp.int32))

    def gather_step(step):
        copies = []
        for way, d in ((0, 1), (1, -1)):
            block = (z + NZ - d * step) % NZ
            if step < 3:
                ref = ctg.at[block]
            else:
                ref = ctg.at[block, pl.ds(way * (TOK // 2), TOK // 2)]
            copies.append(remote(ref, ref, ag_s.at[way, step], ag_r.at[way, step], device(s, xh, (z + NZ + d) % NZ)))
        return copies

    gathers = [gather_step(step) for step in range(4)]
    weights = remote(w_hbm, w2.at[1], w_s, w_r, device(s, 1 - xh, z))

    def inputs_copy(slot, k):
        half = 1 - xh if slot == 0 else xh
        return remote(
            x_hbm.at[:, columns(half, ring(k))], xr.at[slot, z], x_s.at[slot, k], x_r.at[slot, k], device(s, xh, ring(k))
        )

    inputs_copies = [{k: inputs_copy(slot, k) for k in FAR_FIRST} for slot in range(2)]

    def lowered_copy(slot, k):
        half = xh if slot == 0 else 1 - xh
        return remote(lo.at[slot, k], up_out.at[:, columns(half, z)], l_s.at[slot, k], l_r.at[slot, k], device(s - 1, xh, ring(k)))

    crossing = (s > 0) & (s % 2 == 0)

    def relay_copy(slot, k):
        return remote(lo.at[slot, k], passed.at[slot, k], l_s.at[slot, k], r_r.at[slot, k], device(s - 1, xh, z))

    def forward_copy(slot, k):
        half = xh if slot == 0 else 1 - xh
        return remote(
            passed.at[slot, k], up_out.at[:, columns(half, z)], f_s.at[slot, k], l_r.at[slot, k], device(s, xh, ring(k))
        )

    def lowered_send(pairs):
        for slot, k in pairs:
            direct = s > 0
            if k:
                direct = direct & ~(crossing & (GROUP_OF[slot, k] < NZ - s // 2))

            @pl.when(direct)
            def _():
                lowered_copy(slot, k).start()

    def relay_send():
        for i, group in enumerate(GROUPS):

            @pl.when(crossing & (i < NZ - s // 2))
            def _():
                for slot, k in group:
                    relay_copy(slot, k).start()

    def pass_on(first, last, action):
        for i in range(first, last):

            @pl.when((s % 2 == 1) & (i < NZ - (s + 1) // 2))
            def _():
                for slot, k in GROUPS[i]:
                    action(slot, k)

    def pass_start(slot, k):
        relay_copy(slot, k).wait_recv()
        forward_copy(slot, k).start()

    def lowered(slot, k, send=True):
        lo[slot, k] = lax.dot_general(
            ctg[ring(k)], w2[slot], (((1,), (1,)), ((), ())), preferred_element_type=F32
        ).astype(BF)
        if send:
            lowered_send(((slot, k),))

    def send_inputs(step):
        for slot, k in INPUT_ORDER[step]:
            inputs_copies[slot][k].start()

    for copy in gathers[0]:
        copy.start()
    weights.start()
    send_inputs(0)

    zbuf[...] = jnp.zeros_like(zbuf)

    @pl.when(s == LAST)
    def _():
        for i in range(NZ):
            pltpu.make_async_copy(zbuf, up_out.at[:, pl.ds(i * 2 * ROWS, 2 * ROWS)], z_s.at[i]).start()

    loads[2].wait()
    lowered(0, 0)

    for step in range(4):
        for copy in gathers[step]:
            copy.wait_recv()
        if step < 3:
            for copy in gathers[step + 1]:
                copy.start()
        send_inputs(step + 1)
        if step == 2:

            @pl.when(s < LAST)
            def _():
                greet(ready, device(s + 1, xh, z))

        for k in ((step + 1, NZ - 1 - step) if step < 3 else (4,)):
            lowered(0, k, send=False)

    @pl.when(s > 0)
    def _():
        pl.semaphore_wait(ready, 1)

    def gradient(slot, store):
        for part in range(2):
            cols = pl.ds(part * 256, 256)
            xs = xr[slot, :, :, cols].reshape(NZ * TOK, 256)
            ct = ctg[...].reshape(NZ * TOK, FF)
            store(cols, lax.dot_general(xs, ct, (((0,), (0,)), ((), ())), preferred_element_type=F32))

    for copy in inputs_copies[0].values():
        copy.wait_recv()
    loads[3].wait()

    def store_send(rows, value):
        gsend[rows, :] = value.astype(BF)

    gradient(0, store_send)
    partial = remote(gsend, grecv, g_s, g_r, device(s, 1 - xh, z))
    partial.start()

    weights.wait_recv()
    for k in range(NZ):
        lowered(1, k, send=k == 0)
    relay_send()
    lowered_send(ORDER[0:4])

    loads[5].wait()
    loads[6].wait()
    for q in range(4):
        rcol[pl.ds(q * 128, 128), :] = jnp.transpose(jnp.broadcast_to(rvec[pl.ds(q, 1), :], (128, 128)))

    for copy in inputs_copies[1].values():
        copy.wait_recv()
    lowered_send(ORDER[4:7])
    loads[4].wait()

    def store_own(rows, value):
        grad[rows, :] = value

    gradient(1, store_own)
    partial.wait_recv()

    def tile(q):
        return pl.ds(q * 128, 128)

    def fold(v):
        return (v[0:8] + v[8:16]) + (v[16:24] + v[24:32])

    def stats_step(i, carry):
        us, vs, rsum = carry
        rows = pl.ds(pl.multiple_of(i * 32, 32), 32)
        squares = []
        for q in range(8):
            g = grad[rows, tile(q)] + grecv[rows, tile(q)].astype(F32)
            grad[rows, tile(q)] = g
            squares.append(g * g)
        rowsum = ((squares[0] + squares[1]) + (squares[2] + squares[3])) + ((squares[4] + squares[5]) + (squares[6] + squares[7]))
        rowmean = jnp.sum(rowsum, axis=1, keepdims=True) * (1.0 / FF) + TINY_ADD
        rnew = BETA_TWO * rcol[rows, :] + (1.0 - BETA_TWO) * jnp.broadcast_to(rowmean, (32, 128))
        rcol[rows, :] = rnew
        rinv = 1.0 / rnew
        us = tuple(u + fold(sq) for u, sq in zip(us, squares))
        vs = tuple(v + fold(sq * rinv) for v, sq in zip(vs, squares))
        return us, vs, rsum + fold(rnew)

    zero = jnp.zeros((8, 128), F32)
    us, vs, rsum = lax.fori_loop(0, ROWS // 32, stats_step, ((zero,) * 8, (zero,) * 8, zero))
    rsum = jnp.sum(rsum, axis=0, keepdims=True)
    for q in range(8):
        smine[q, 0:1] = jnp.sum(us[q], axis=0, keepdims=True) + ROWS * TINY_ADD
        smine[q, 1:2] = jnp.sum(vs[q], axis=0, keepdims=True)
        smine[q, 2:3] = rsum
        smine[q, 3:4] = rsum

    sums = []
    for other in range(2):
        half = 1 - xh if other else xh
        for k in FAR_FIRST + ((0,) if other else ()):
            sums.append(remote(smine.at[ring(k)], sred.at[xh, z], s_s.at[other, k], s_r.at[other, k], device(s, half, ring(k))))
    for copy in sums:
        copy.start()
    lowered_send(ORDER[7:10])
    pass_on(0, 4, pass_start)
    sred[xh, z] = smine[z]
    for q in range(4):
        row_out[pl.ds(q, 1), :] = jnp.transpose(rcol[pl.ds(q * 128, 128), :])[0:1, :]
    for copy in sums:
        copy.wait_recv()
    total = sred[0, 0]
    for i in range(1, 2 * NZ):
        total = total + sred[i // NZ, i % NZ]
    cnew = BETA_TWO * cvec[pl.ds(z, 1), :] + (1.0 - BETA_TWO) * (total[0:1] * (1.0 / D))
    sgat[z, 0:1] = cnew
    sgat[z, 1:2] = total[1:2] / cnew
    shares = [remote(sgat.at[z], sgat.at[z], p_s.at[k], p_r.at[k], device(s, xh, ring(k))) for k in FAR_FIRST]
    for copy in shares:
        copy.start()
    pass_on(4, NZ, pass_start)
    lowered_send(ORDER[10:14])
    average = total[2:3] * (1.0 / D)
    for copy in shares:
        copy.wait_recv()
    ratio = sgat[0, 1:2]
    for i in range(1, NZ):
        ratio = ratio + sgat[i, 1:2]
    ratio = jnp.broadcast_to(jnp.sum(ratio, axis=1, keepdims=True), (1, 128))
    root = jnp.sqrt(ratio * average * (1.0 / (float(D) * float(FF))))
    scale = jnp.sqrt(average) / jnp.maximum(1.0, root)
    colfac = []
    for q in range(NZ):
        col_out[pl.ds(q, 1), :] = sgat[q, 0:1]
        colfac.append(jnp.broadcast_to(lax.rsqrt(sgat[q, 0:1]), (32, 128)))

    def update_step(i, carry):
        rows = pl.ds(pl.multiple_of(i * 32, 32), 32)
        rowfac = lax.rsqrt(rcol[rows, :]) * scale
        for q in range(8):
            step_out[rows, tile(q)] = (grad[rows, tile(q)] * rowfac * colfac[q]).astype(BF)
        return carry

    lax.fori_loop(0, ROWS // 32, update_step, 0)

    for copies in gathers:
        for copy in copies:
            copy.wait_send()
    weights.wait_send()
    for copies in inputs_copies:
        for copy in copies.values():
            copy.wait_send()
    partial.wait_send()
    for copy in sums + shares:
        copy.wait_send()

    @pl.when(s > 0)
    def _():
        for slot in range(2):
            for k in range(NZ):
                lowered_copy(slot, k).wait_send()

    pass_on(0, NZ, lambda slot, k: forward_copy(slot, k).wait_send())

    @pl.when(s < LAST)
    def _():
        for slot in range(2):
            for k in range(NZ):
                lowered_copy(slot, k).wait_recv()

    @pl.when(s == LAST)
    def _():
        for i in range(NZ):
            pltpu.make_async_copy(zbuf, up_out.at[:, pl.ds(i * 2 * ROWS, 2 * ROWS)], z_s.at[i]).wait()


def place(*refs):
    ins, outs, sem = refs[:4], refs[4:8], refs[8]
    copies = [pltpu.make_async_copy(a, b, sem.at[i]) for i, (a, b) in enumerate(zip(ins, outs))]
    for copy in copies:
        copy.start()
    for copy in copies:
        copy.wait()


def local(inputs, hidden_grad, gate_pre, up_weight, row_state, col_state):
    hbm = pl.BlockSpec(memory_space=pl.ANY)
    dma = pltpu.SemaphoreType.DMA
    upstream, step_out, row_new, col_new = pl.pallas_call(
        body,
        name="relay_step",
        out_shape=(
            jax.ShapeDtypeStruct((TOK, D), BF),
            jax.ShapeDtypeStruct((ROWS, FF), BF),
            jax.ShapeDtypeStruct((ROWS // 128, 128), F32),
            jax.ShapeDtypeStruct((FF // 128, 128), F32),
        ),
        in_specs=[hbm] * 6,
        out_specs=(hbm,) + (pl.BlockSpec(memory_space=pltpu.VMEM),) * 3,
        scratch_shapes=[
            pltpu.VMEM((TOK, FF), BF),
            pltpu.VMEM((TOK, FF), BF),
            pltpu.VMEM((NZ, TOK, FF), BF),
            pltpu.VMEM((2, ROWS, FF), BF),
            pltpu.VMEM((2, NZ, TOK, ROWS), BF),
            pltpu.VMEM((2, NZ, TOK, ROWS), BF),
            pltpu.VMEM((ROWS, FF), F32),
            pltpu.VMEM((ROWS, FF), BF),
            pltpu.VMEM((ROWS, FF), BF),
            pltpu.VMEM((ROWS, 128), F32),
            pltpu.VMEM((ROWS // 128, 128), F32),
            pltpu.VMEM((FF // 128, 128), F32),
            pltpu.VMEM((NZ, 4, 128), F32),
            pltpu.VMEM((2, NZ, 4, 128), F32),
            pltpu.VMEM((NZ, 2, 128), F32),
            pltpu.VMEM((TOK, 2 * ROWS), BF),
            pltpu.VMEM((2, NZ, TOK, ROWS), BF),
            dma((7,)),
            dma((2, 4)), dma((2, 4)),
            dma(()), dma(()),
            dma((2, NZ)), dma((2, NZ)),
            dma((2, NZ)), dma((2, NZ)),
            dma(()), dma(()),
            dma((NZ,)), dma((NZ,)),
            dma((2, NZ)), dma((2, NZ)),
            dma((NZ,)),
            dma((2, NZ)), dma((2, NZ)),
            pltpu.SemaphoreType.REGULAR,
        ],
        compiler_params=pltpu.CompilerParams(collective_id=0, has_side_effects=True, vmem_limit_bytes=32 << 20),
        cost_estimate=pl.CostEstimate(flops=4 * 1024 * 1024 * 1024, transcendentals=TOK * FF, bytes_accessed=8 << 20),
    )(
        *(
            pltpu.with_memory_space_constraint(v, pltpu.HBM)
            for v in (inputs, hidden_grad, gate_pre, up_weight, row_state.reshape(ROWS // 128, 128), col_state.reshape(FF // 128, 128))
        )
    )
    results = (upstream, step_out, row_new, col_new)
    upstream, step_out, row_new, col_new = pl.pallas_call(
        place,
        name="place_outputs",
        out_shape=tuple(jax.ShapeDtypeStruct(v.shape, v.dtype) for v in results),
        in_specs=[hbm] * 4,
        out_specs=tuple([pl.BlockSpec(memory_space=pltpu.HBM)] * 4),
        scratch_shapes=[dma((4,))],
        compiler_params=pltpu.CompilerParams(vmem_limit_bytes=1 << 20),
    )(*results)
    return upstream, step_out, row_new.reshape(ROWS), col_new.reshape(FF)


def solution(mesh):
    rows = P(("section", "dp"), None)
    placed = (rows, rows, rows, rows, P(("section", "dp")), P("section"))
    return jax.shard_map(
        local,
        mesh=mesh,
        in_specs=placed,
        out_specs=(rows, rows, P(("section", "dp")), P("section")),
        check_vma=False,
    )
```

```python
import functools

import jax
import jax.numpy as jnp
from jax import lax
from jax.experimental import pallas as pl
from jax.experimental.pallas import tpu as pltpu
from jax.sharding import PartitionSpec as P

D = 8192
FF = 1024
TOK = 128
ROWS = 512
NZ = 8
BETA_TWO = 0.75
TINY_ADD = 1e-30
LAST = 15

GROUPS = (
    ((0, 4),), ((1, 4),), ((0, 3), (0, 1)), ((0, 5), (0, 7)), ((1, 3), (1, 1)), ((1, 5), (1, 7)), ((0, 2), (0, 6)), ((1, 2), (1, 6)),
)
GROUP_OF = {pair: i for i, group in enumerate(GROUPS) for pair in group}

MESH = pl.DeviceIdType.MESH
BF = jnp.bfloat16
F32 = jnp.float32

NEAR_FIRST = (1, 7, 2, 6, 3, 5, 4)
FAR_FIRST = (4, 3, 5, 2, 6, 1, 7)
INPUT_ORDER = (((0, 1), (0, 7), (1, 1), (1, 7)), ((0, 2), (0, 6)), ((0, 3), (0, 5)), ((0, 4), (1, 4), (1, 3), (1, 5), (1, 2), (1, 6)), ())
ORDER = tuple((slot, k) for slot in range(2) for k in FAR_FIRST)


def body(
    x_hbm, hg_hbm, gp_hbm, w_hbm, rstate_hbm, cstate_hbm,
    up_out, step_out, row_out, col_out,
    hg, gp, ctg, w2, xr, lo, grad, gsend, grecv, rcol, rvec, cvec, smine, sred, sgat, zbuf, passed,
    lsem, ag_s, ag_r, w_s, w_r, x_s, x_r, l_s, l_r, g_s, g_r, p_s, p_r, s_s, s_r, z_s, r_r, f_s, ready,
):
    s = lax.axis_index("section")
    dp = lax.axis_index("dp")
    xh, z = dp // NZ, dp % NZ

    def ring(k):
        return (z + k) % NZ

    def device(section, half, zz):
        return {"section": section, "dp": half * NZ + zz}

    def remote(src, dst, send, recv, target):
        return pltpu.make_async_remote_copy(
            src_ref=src, dst_ref=dst, send_sem=send, recv_sem=recv, device_id=target, device_id_type=MESH
        )

    barrier = pltpu.get_barrier_semaphore()
    def greet(sem, target):
        pl.semaphore_signal(sem, inc=1, device_id=target, device_id_type=MESH)

    for k in (1, NZ - 1):
        greet(barrier, device(s, xh, ring(k)))
    greet(barrier, device(s, 1 - xh, z))

    @pl.when(s < LAST)
    def _():
        greet(barrier, device(s + 1, xh, z))

    @pl.when(s > 0)
    def _():
        greet(barrier, device(s - 1, xh, z))

    def columns(half, zz):
        return pl.ds(pl.multiple_of((half * NZ + zz) * ROWS, ROWS), ROWS)

    loads = [
        pltpu.make_async_copy(hg_hbm, hg, lsem.at[0]),
        pltpu.make_async_copy(gp_hbm, gp, lsem.at[1]),
        pltpu.make_async_copy(w_hbm, w2.at[0], lsem.at[2]),
        pltpu.make_async_copy(x_hbm.at[:, columns(1 - xh, z)], xr.at[0, z], lsem.at[3]),
        pltpu.make_async_copy(x_hbm.at[:, columns(xh, z)], xr.at[1, z], lsem.at[4]),
        pltpu.make_async_copy(rstate_hbm, rvec, lsem.at[5]),
        pltpu.make_async_copy(cstate_hbm, cvec, lsem.at[6]),
    ]
    for load in loads:
        load.start()
    loads[0].wait()
    loads[1].wait()

    @pl.loop(0, 4)
    def _(i):
        rows = pl.ds(pl.multiple_of(i * 32, 32), 32)
        v = gp[rows, :].astype(F32)
        ctg[z, rows, :] = (hg[rows, :].astype(F32) * (v / (1.0 + jnp.exp(-v)))).astype(BF)

    pl.semaphore_wait(barrier, 3 + (s > 0).astype(jnp.int32) + (s < LAST).astype(jnp.int32))

    def gather_step(step):
        copies = []
        for way, d in ((0, 1), (1, -1)):
            block = (z + NZ - d * step) % NZ
            if step < 3:
                ref = ctg.at[block]
            else:
                ref = ctg.at[block, pl.ds(way * (TOK // 2), TOK // 2)]
            copies.append(remote(ref, ref, ag_s.at[way, step], ag_r.at[way, step], device(s, xh, (z + NZ + d) % NZ)))
        return copies

    gathers = [gather_step(step) for step in range(4)]
    weights = remote(w_hbm, w2.at[1], w_s, w_r, device(s, 1 - xh, z))

    def inputs_copy(slot, k):
        half = 1 - xh if slot == 0 else xh
        return remote(
            x_hbm.at[:, columns(half, ring(k))], xr.at[slot, z], x_s.at[slot, k], x_r.at[slot, k], device(s, xh, ring(k))
        )

    inputs_copies = [{k: inputs_copy(slot, k) for k in FAR_FIRST} for slot in range(2)]

    def lowered_copy(slot, k):
        half = xh if slot == 0 else 1 - xh
        return remote(lo.at[slot, k], up_out.at[:, columns(half, z)], l_s.at[slot, k], l_r.at[slot, k], device(s - 1, xh, ring(k)))

    crossing = (s > 0) & (s % 2 == 0)

    def relay_copy(slot, k):
        return remote(lo.at[slot, k], passed.at[slot, k], l_s.at[slot, k], r_r.at[slot, k], device(s - 1, xh, z))

    def forward_copy(slot, k):
        half = xh if slot == 0 else 1 - xh
        return remote(
            passed.at[slot, k], up_out.at[:, columns(half, z)], f_s.at[slot, k], l_r.at[slot, k], device(s, xh, ring(k))
        )

    def lowered_send(pairs):
        for slot, k in pairs:
            direct = s > 0
            if k:
                direct = direct & ~(crossing & (GROUP_OF[slot, k] < NZ - s // 2))

            @pl.when(direct)
            def _():
                lowered_copy(slot, k).start()

    def relay_send():
        for i, group in enumerate(GROUPS):

            @pl.when(crossing & (i < NZ - s // 2))
            def _():
                for slot, k in group:
                    relay_copy(slot, k).start()

    def pass_on(first, last, action):
        for i in range(first, last):

            @pl.when((s % 2 == 1) & (i < NZ - (s + 1) // 2))
            def _():
                for slot, k in GROUPS[i]:
                    action(slot, k)

    def pass_start(slot, k):
        relay_copy(slot, k).wait_recv()
        forward_copy(slot, k).start()

    def lowered(slot, k, send=True):
        lo[slot, k] = lax.dot_general(
            ctg[ring(k)], w2[slot], (((1,), (1,)), ((), ())), preferred_element_type=F32
        ).astype(BF)
        if send:
            lowered_send(((slot, k),))

    def send_inputs(step):
        for slot, k in INPUT_ORDER[step]:
            inputs_copies[slot][k].start()

    for copy in gathers[0]:
        copy.start()
    weights.start()
    send_inputs(0)

    zbuf[...] = jnp.zeros_like(zbuf)

    @pl.when(s == LAST)
    def _():
        for i in range(NZ):
            pltpu.make_async_copy(zbuf, up_out.at[:, pl.ds(i * 2 * ROWS, 2 * ROWS)], z_s.at[i]).start()

    loads[2].wait()
    lowered(0, 0)

    for step in range(4):
        for copy in gathers[step]:
            copy.wait_recv()
        if step < 3:
            for copy in gathers[step + 1]:
                copy.start()
        send_inputs(step + 1)
        if step == 2:

            @pl.when(s < LAST)
            def _():
                greet(ready, device(s + 1, xh, z))

        for k in ((step + 1, NZ - 1 - step) if step < 3 else (4,)):
            lowered(0, k, send=False)

    @pl.when(s > 0)
    def _():
        pl.semaphore_wait(ready, 1)

    def gradient(slot, store):
        for part in range(2):
            cols = pl.ds(part * 256, 256)
            xs = xr[slot, :, :, cols].reshape(NZ * TOK, 256)
            ct = ctg[...].reshape(NZ * TOK, FF)
            store(cols, lax.dot_general(xs, ct, (((0,), (0,)), ((), ())), preferred_element_type=F32))

    for copy in inputs_copies[0].values():
        copy.wait_recv()
    loads[3].wait()

    def store_send(rows, value):
        gsend[rows, :] = value.astype(BF)

    gradient(0, store_send)
    partial = remote(gsend, grecv, g_s, g_r, device(s, 1 - xh, z))
    partial.start()

    weights.wait_recv()
    for k in range(NZ):
        lowered(1, k, send=k == 0)
    relay_send()
    lowered_send(ORDER[0:4])

    loads[5].wait()
    loads[6].wait()
    for q in range(4):
        rcol[pl.ds(q * 128, 128), :] = jnp.transpose(jnp.broadcast_to(rvec[pl.ds(q, 1), :], (128, 128)))

    for copy in inputs_copies[1].values():
        copy.wait_recv()
    lowered_send(ORDER[4:7])
    loads[4].wait()

    def store_own(rows, value):
        grad[rows, :] = value

    gradient(1, store_own)
    partial.wait_recv()

    def tile(q):
        return pl.ds(q * 128, 128)

    def fold(v):
        return (v[0:8] + v[8:16]) + (v[16:24] + v[24:32])

    def stats_step(i, carry):
        us, vs, rsum = carry
        rows = pl.ds(pl.multiple_of(i * 32, 32), 32)
        squares = []
        for q in range(8):
            g = grad[rows, tile(q)] + grecv[rows, tile(q)].astype(F32)
            grad[rows, tile(q)] = g
            squares.append(g * g)
        rowsum = ((squares[0] + squares[1]) + (squares[2] + squares[3])) + ((squares[4] + squares[5]) + (squares[6] + squares[7]))
        rowmean = jnp.sum(rowsum, axis=1, keepdims=True) * (1.0 / FF) + TINY_ADD
        rnew = BETA_TWO * rcol[rows, :] + (1.0 - BETA_TWO) * jnp.broadcast_to(rowmean, (32, 128))
        rcol[rows, :] = rnew
        rinv = 1.0 / rnew
        us = tuple(u + fold(sq) for u, sq in zip(us, squares))
        vs = tuple(v + fold(sq * rinv) for v, sq in zip(vs, squares))
        return us, vs, rsum + fold(rnew)

    zero = jnp.zeros((8, 128), F32)
    us, vs, rsum = lax.fori_loop(0, ROWS // 32, stats_step, ((zero,) * 8, (zero,) * 8, zero))
    rsum = jnp.sum(rsum, axis=0, keepdims=True)
    for q in range(8):
        smine[q, 0:1] = jnp.sum(us[q], axis=0, keepdims=True) + ROWS * TINY_ADD
        smine[q, 1:2] = jnp.sum(vs[q], axis=0, keepdims=True)
        smine[q, 2:3] = rsum
        smine[q, 3:4] = rsum

    sums = []
    for other in range(2):
        half = 1 - xh if other else xh
        for k in FAR_FIRST + ((0,) if other else ()):
            sums.append(remote(smine.at[ring(k)], sred.at[xh, z], s_s.at[other, k], s_r.at[other, k], device(s, half, ring(k))))
    for copy in sums:
        copy.start()
    lowered_send(ORDER[7:10])
    pass_on(0, 4, pass_start)
    sred[xh, z] = smine[z]
    for q in range(4):
        row_out[pl.ds(q, 1), :] = jnp.transpose(rcol[pl.ds(q * 128, 128), :])[0:1, :]
    for copy in sums:
        copy.wait_recv()
    total = sred[0, 0]
    for i in range(1, 2 * NZ):
        total = total + sred[i // NZ, i % NZ]
    cnew = BETA_TWO * cvec[pl.ds(z, 1), :] + (1.0 - BETA_TWO) * (total[0:1] * (1.0 / D))
    sgat[z, 0:1] = cnew
    sgat[z, 1:2] = total[1:2] / cnew
    shares = [remote(sgat.at[z], sgat.at[z], p_s.at[k], p_r.at[k], device(s, xh, ring(k))) for k in FAR_FIRST]
    for copy in shares:
        copy.start()
    lowered_send(ORDER[10:14])
    pass_on(4, NZ, pass_start)
    average = total[2:3] * (1.0 / D)
    for copy in shares:
        copy.wait_recv()
    ratio = sgat[0, 1:2]
    for i in range(1, NZ):
        ratio = ratio + sgat[i, 1:2]
    ratio = jnp.broadcast_to(jnp.sum(ratio, axis=1, keepdims=True), (1, 128))
    root = jnp.sqrt(ratio * average * (1.0 / (float(D) * float(FF))))
    scale = jnp.sqrt(average) / jnp.maximum(1.0, root)
    colfac = []
    for q in range(NZ):
        col_out[pl.ds(q, 1), :] = sgat[q, 0:1]
        colfac.append(jnp.broadcast_to(lax.rsqrt(sgat[q, 0:1]), (32, 128)))

    def update_step(i, carry):
        rows = pl.ds(pl.multiple_of(i * 32, 32), 32)
        rowfac = lax.rsqrt(rcol[rows, :]) * scale
        for q in range(8):
            step_out[rows, tile(q)] = (grad[rows, tile(q)] * rowfac * colfac[q]).astype(BF)
        return carry

    lax.fori_loop(0, ROWS // 32, update_step, 0)

    for copies in gathers:
        for copy in copies:
            copy.wait_send()
    weights.wait_send()
    for copies in inputs_copies:
        for copy in copies.values():
            copy.wait_send()
    partial.wait_send()
    for copy in sums + shares:
        copy.wait_send()

    @pl.when(s > 0)
    def _():
        for slot in range(2):
            for k in range(NZ):
                lowered_copy(slot, k).wait_send()

    pass_on(0, NZ, lambda slot, k: forward_copy(slot, k).wait_send())

    @pl.when(s < LAST)
    def _():
        for slot in range(2):
            for k in range(NZ):
                lowered_copy(slot, k).wait_recv()

    @pl.when(s == LAST)
    def _():
        for i in range(NZ):
            pltpu.make_async_copy(zbuf, up_out.at[:, pl.ds(i * 2 * ROWS, 2 * ROWS)], z_s.at[i]).wait()


def place(*refs):
    ins, outs, sem = refs[:4], refs[4:8], refs[8]
    copies = [pltpu.make_async_copy(a, b, sem.at[i]) for i, (a, b) in enumerate(zip(ins, outs))]
    for copy in copies:
        copy.start()
    for copy in copies:
        copy.wait()


def local(inputs, hidden_grad, gate_pre, up_weight, row_state, col_state):
    hbm = pl.BlockSpec(memory_space=pl.ANY)
    dma = pltpu.SemaphoreType.DMA
    upstream, step_out, row_new, col_new = pl.pallas_call(
        body,
        name="relay_step",
        out_shape=(
            jax.ShapeDtypeStruct((TOK, D), BF),
            jax.ShapeDtypeStruct((ROWS, FF), BF),
            jax.ShapeDtypeStruct((ROWS // 128, 128), F32),
            jax.ShapeDtypeStruct((FF // 128, 128), F32),
        ),
        in_specs=[hbm] * 6,
        out_specs=(hbm,) + (pl.BlockSpec(memory_space=pltpu.VMEM),) * 3,
        scratch_shapes=[
            pltpu.VMEM((TOK, FF), BF),
            pltpu.VMEM((TOK, FF), BF),
            pltpu.VMEM((NZ, TOK, FF), BF),
            pltpu.VMEM((2, ROWS, FF), BF),
            pltpu.VMEM((2, NZ, TOK, ROWS), BF),
            pltpu.VMEM((2, NZ, TOK, ROWS), BF),
            pltpu.VMEM((ROWS, FF), F32),
            pltpu.VMEM((ROWS, FF), BF),
            pltpu.VMEM((ROWS, FF), BF),
            pltpu.VMEM((ROWS, 128), F32),
            pltpu.VMEM((ROWS // 128, 128), F32),
            pltpu.VMEM((FF // 128, 128), F32),
            pltpu.VMEM((NZ, 4, 128), F32),
            pltpu.VMEM((2, NZ, 4, 128), F32),
            pltpu.VMEM((NZ, 2, 128), F32),
            pltpu.VMEM((TOK, 2 * ROWS), BF),
            pltpu.VMEM((2, NZ, TOK, ROWS), BF),
            dma((7,)),
            dma((2, 4)), dma((2, 4)),
            dma(()), dma(()),
            dma((2, NZ)), dma((2, NZ)),
            dma((2, NZ)), dma((2, NZ)),
            dma(()), dma(()),
            dma((NZ,)), dma((NZ,)),
            dma((2, NZ)), dma((2, NZ)),
            dma((NZ,)),
            dma((2, NZ)), dma((2, NZ)),
            pltpu.SemaphoreType.REGULAR,
        ],
        compiler_params=pltpu.CompilerParams(collective_id=0, has_side_effects=True, vmem_limit_bytes=32 << 20),
        cost_estimate=pl.CostEstimate(flops=4 * 1024 * 1024 * 1024, transcendentals=TOK * FF, bytes_accessed=8 << 20),
    )(
        *(
            pltpu.with_memory_space_constraint(v, pltpu.HBM)
            for v in (inputs, hidden_grad, gate_pre, up_weight, row_state.reshape(ROWS // 128, 128), col_state.reshape(FF // 128, 128))
        )
    )
    results = (upstream, step_out, row_new, col_new)
    upstream, step_out, row_new, col_new = pl.pallas_call(
        place,
        name="place_outputs",
        out_shape=tuple(jax.ShapeDtypeStruct(v.shape, v.dtype) for v in results),
        in_specs=[hbm] * 4,
        out_specs=tuple([pl.BlockSpec(memory_space=pltpu.HBM)] * 4),
        scratch_shapes=[dma((4,))],
        compiler_params=pltpu.CompilerParams(vmem_limit_bytes=1 << 20),
    )(*results)
    return upstream, step_out, row_new.reshape(ROWS), col_new.reshape(FF)


def solution(mesh):
    rows = P(("section", "dp"), None)
    placed = (rows, rows, rows, rows, P(("section", "dp")), P("section"))
    return jax.shard_map(
        local,
        mesh=mesh,
        in_specs=placed,
        out_specs=(rows, rows, P(("section", "dp")), P("section")),
        check_vma=False,
    )
```
